1024 devices in a mesh: gx: 16 (over y, core), yz: 64 (over x, z).
Axes of the slice: x: 8, y: 8, z: 8, core: 2. Of those that a mesh axis runs over, the one named last changes fastest.
Arguments:
- gas: float32 [10, 32, 256, 128], P(None, 'gx', 'yz'), may hold values from -6 to 6
- kappa: float32 [32, 256, 128], P('gx', 'yz'), may hold values from 0.01 to 0.06
- velocity: float32 [32, 256, 128], P('gx', 'yz'), may hold values from 0.1 to 0.6
- drop_mass: float32 [32768, 128], P(('gx', 'yz')), may hold values from 0.2 to 2
- drop_temp: float32 [32768, 128], P(('gx', 'yz')), may hold values from -6 to 6
- block_fill: int32 [32768], P(('gx', 'yz')), may hold values from 1 to 128
- drop_cell: int32 [32768, 128], P(('gx', 'yz')), may hold values from 0 to 1023
- block_dest: int32 [32768, 1], P(('gx', 'yz')), may hold values from 0 to 63; in each aligned block of 32 rows (0 to 31, 32 to 63, ...) at most 2 rows name the same one
Outputs:
- gas_next: float32 [10, 32, 256, 128], P(None, 'gx', 'yz')
- mass_next: float32 [32768, 128], P(('gx', 'yz'))
- temp_next: float32 [32768, 128], P(('gx', 'yz'))
The draws below stay inside these ranges and needn't reach their ends.
Inputs may be any that keep to these rules, and one draw needn't show every extreme that they name: `block_dest`: among the blocks of one device, at most 2 name the same brick, and in every draw some device sends exactly 2 blocks to some brick.
All inputs are finite; a program needn't handle non-finite values.
Results may differ from the reference program's by a relative error of at most 0.00007.
Values sent between devices are 32-bit elements; how exact they have to be, the bound alone decides.
A program may use at most 32 MiB of HBM per device.

```python
import math
import jax
import jax.numpy as jnp
import numpy as np
from jax import lax

FIELDS = 10
DROPS = 128
SUBSTEPS = 4
CX = 2
CY = 4
CZ = 128
BLK_DEV = 32
CAP = 2
NX = 32
NY = 256
BLOCKS = 32768
N_YZ = 64


def with_ends(entries, rng, smallest, top_value):
    index_at = [jax.random.randint(jax.random.fold_in(rng, axis), (), 0, length) for axis, length in enumerate(entries.shape)]
    longest = entries.shape.index(max(entries.shape))
    next_to = index_at[:longest] + [(index_at[longest] + 1) % entries.shape[longest]] + index_at[longest + 1:]
    return entries.at[tuple(index_at)].set(smallest).at[tuple(next_to)].set(top_value)


def level_of(key, dims, cuts, least, largest):
    def one(position, parts):
        heights = jax.random.uniform(jax.random.fold_in(jax.random.fold_in(key, 6), position), (parts,), jnp.float32, least / len(cuts), largest / len(cuts))
        return jnp.repeat(jnp.exp(heights), dims[position] // parts).reshape((-1,) + (1,) * (len(dims) - position - 1))

    level = one(*cuts[0])
    for cut in cuts[1:]:
        level = level * one(*cut)
    return level


def deal_out(own_key, own, number, rows, amount, top, most, skew):
    order = jax.random.permutation(own_key, amount)
    heavy_load, common = portions_of(amount, rows * top, most, skew, True), portions_of(amount, rows * top, most, skew, False)
    places = jnp.arange(amount)

    def named(lengths, turn):
        used = int((lengths > 0).sum())
        fixed = max(1, used // 4)
        passed = fixed + (places - fixed + turn * (used - fixed)) % max(1, amount - fixed)
        return jnp.zeros((amount,), jnp.int32).at[order[jnp.where(places < fixed, places, passed)]].set(jnp.asarray(lengths, jnp.int32))

    lengths = jnp.where(number % 4 == 0, named(heavy_load, number // 4), named(common, number - number // 4 - 1))
    mixed = jax.random.permutation(jax.random.fold_in(own, 3), amount)
    source_of, sink = mixed[0:amount // 2 * 2:2], mixed[1:amount // 2 * 2:2]
    room = jnp.minimum(lengths[source_of] - 1, most - lengths[sink]) // 2
    room = jnp.where((source_of == order[0]) | (sink == order[0]) | (lengths[sink] == 0), 0, jnp.maximum(room, 0))
    passed = jax.random.randint(jax.random.fold_in(own, 4), (amount // 2,), 0, 1 << 20) % (room + 1)
    lengths = lengths.at[source_of].add(-passed).at[sink].add(passed)
    labels = jnp.searchsorted(jnp.cumsum(lengths), jnp.arange(rows * top), side="right").astype(jnp.int32)
    table = labels.reshape(top, rows).T
    table = table[jax.random.permutation(jax.random.fold_in(own, 1), rows)]
    turn = jax.random.randint(jax.random.fold_in(own, 2), (rows, 1), 0, top)
    return jnp.take_along_axis(table, (jnp.arange(top)[None, :] + turn) % top, axis=1)


def portions_of(count, total, bound, slope, full):
    portions = [(1 << 20) // math.isqrt(grade ** slope) + 1 for grade in range(1, count + 1)]
    largest = bound if full else min(bound, max(-(-total // count), total * portions[0] // sum(portions)))
    least = 1 if total - largest >= count - 1 else 0
    counts, surplus = [largest] + [least] * (count - 1), total - largest - least * (count - 1)
    while surplus > 0:
        movable = [i for i in range(1, count) if counts[i] < largest] or [i for i in range(1, count) if counts[i] < bound]
        pool, budget = sum([portions[i] for i in movable]), surplus
        for i in movable:
            addition = min(bound - counts[i], max(1, budget * portions[i] // pool), surplus)
            counts[i] = counts[i] + addition
            surplus = surplus - addition
    return np.array(counts)


def normal_values(own_key, shape, scale, bound, shards=(), kind=jnp.bfloat16):
    result = jax.random.normal(own_key, shape, jnp.float32) * scale
    if len(shards) > 0:
        result = level_of(own_key, shape, shards, -0.22, 0.18) * result
    return jnp.clip(result, min=-bound, max=bound).astype(kind)


def setup_inputs(seed: int = 0) -> dict:
    keys = jax.random.split(jax.random.key(seed), 9)
    gas = normal_values(keys[0], (FIELDS, NX, NY, CZ), 1.0, 6.0, ((1, 16), (2, 64)), jnp.float32)
    kappa = jnp.clip(jnp.exp(math.log(0.06) - 1.7917595 * jax.random.uniform(keys[1], (NX, NY, CZ), jnp.float32) ** level_of(keys[1], (NX, NY, CZ), ((0, 16), (1, 64)), -0.2, 0.2)), 0.01, 0.06)
    velocity = jnp.clip(0.1 + 0.5 * jax.random.uniform(keys[2], (NX, NY, CZ), jnp.float32) ** level_of(keys[2], (NX, NY, CZ), ((0, 16), (1, 64)), -0.2, 0.2), 0.1, 0.6)
    drop_mass = jnp.clip(jnp.exp(math.log(2.0) - 2.3025851 * jax.random.uniform(keys[3], (BLOCKS, DROPS), jnp.float32) ** level_of(keys[3], (BLOCKS, DROPS), ((0, 1024),), -0.2, 0.2)), 0.2, 2.0)
    drop_temp = normal_values(keys[4], (BLOCKS, DROPS), 1.0, 6.0, ((0, 1024),), jnp.float32)
    block_fill = with_ends(jax.random.randint(keys[5], (BLOCKS,), 1, DROPS + 1), jax.random.fold_in(keys[5], 1), 1, DROPS).astype(jnp.int32)
    drop_cell = with_ends(jax.random.randint(keys[6], (BLOCKS, DROPS), 0, CX * CY * CZ), jax.random.fold_in(keys[6], 1), 0, (CX * CY * CZ) - 1).astype(jnp.int32)
    block_dest_keys = jax.random.split(jax.random.fold_in(keys[7], 1), BLOCKS // BLK_DEV)
    block_dest_turns = jax.random.permutation(jax.random.fold_in(keys[7], 3), BLOCKS // BLK_DEV)
    block_dest = jax.vmap(lambda own, number: deal_out(jax.random.fold_in(keys[7], 2), own, number, BLK_DEV, N_YZ, 1, CAP, 2))(block_dest_keys, block_dest_turns).reshape((BLOCKS, 1))
    return {"gas": gas, "kappa": kappa, "velocity": velocity, "drop_mass": drop_mass, "drop_temp": drop_temp, "block_fill": block_fill, "drop_cell": drop_cell, "block_dest": block_dest}


evap_coef = 0.3
heat_coef = 0.8
latent_coef = 0.5
drop_dt = 0.25


def droplet_step(mass_now, temp_now, fuel_gas, temp_gas, living):
    src_mass = jnp.zeros_like(mass_now)
    src_energy = jnp.zeros_like(mass_now)
    for substep in range(SUBSTEPS):
        evap_rate = evap_coef * jax.nn.softplus(temp_now - fuel_gas)
        heat_flow = heat_coef * (temp_gas - temp_now)
        shrunk = mass_now * jnp.exp(-drop_dt * evap_rate)
        src_mass = src_mass + (mass_now - shrunk)
        src_energy = src_energy - drop_dt * heat_flow * mass_now
        temp_now = temp_now + drop_dt * (heat_flow - latent_coef * evap_rate)
        mass_now = shrunk
    zero = jnp.zeros_like(mass_now)
    return (jnp.where(living, mass_now, zero), jnp.where(living, temp_now, zero),
            jnp.where(living, src_mass, zero), jnp.where(living, src_energy, zero))


def transport(field, kappa, velocity):
    padded = jnp.pad(field, ((1, 1), (1, 1), (0, 0)))
    edged = jnp.concatenate([field[:, :, :1], field, field[:, :, -1:]], axis=2)
    beside_all = padded[2:, 1:-1] + padded[:-2, 1:-1] + padded[1:-1, 2:] + padded[1:-1, :-2]
    beside_all = beside_all + edged[:, :, 2:] + edged[:, :, :-2]
    return field + kappa * (beside_all - 6.0 * field) - velocity * (field - padded[:-2, 1:-1])


def reference(gas, kappa, velocity, drop_mass, drop_temp, block_fill, drop_cell, block_dest):
    nfield = gas.shape[0]
    nblock = drop_mass.shape[0]
    lane_ids = jnp.arange(drop_mass.shape[1], dtype=jnp.int32)
    living = lane_ids[None, :] < block_fill[:, None]
    device = jnp.arange(nblock, dtype=jnp.int32) // BLK_DEV
    brick_row = device // N_YZ
    target = block_dest[:, 0]
    local_x = drop_cell // (CY * CZ)
    local_y = (drop_cell // CZ) % CY
    local_z = drop_cell % CZ
    global_x = brick_row[:, None] * CX + local_x
    global_y = target[:, None] * CY + local_y
    flat_cell = ((global_x * NY + global_y) * CZ + local_z).astype(jnp.int32)
    fuel_gas = gas[0].reshape(-1)[flat_cell]
    temp_gas = gas[nfield - 1].reshape(-1)[flat_cell]
    mass_next, temp_next, src_mass, src_energy = droplet_step(drop_mass, drop_temp, fuel_gas, temp_gas, living)
    total = NX * NY * CZ
    dep_mass = jnp.zeros((total,), jnp.float32).at[flat_cell.reshape(-1)].add(src_mass.reshape(-1))
    dep_energy = jnp.zeros((total,), jnp.float32).at[flat_cell.reshape(-1)].add(src_energy.reshape(-1))
    transported = lax.map(lambda field: transport(field, kappa, velocity), gas)
    gas_next = transported.at[0].add(dep_mass.reshape(NX, NY, CZ))
    gas_next = gas_next.at[nfield - 1].add(dep_energy.reshape(NX, NY, CZ))
    return gas_next, mass_next, temp_next
```

```python
import functools
import math

import jax
import jax.numpy as jnp
from jax import lax
from jax.experimental import pallas as pl
from jax.experimental.pallas import tpu as pltpu
from jax.sharding import PartitionSpec as P

SUBSTEPS = 4
evap_coef = 0.3
heat_coef = 0.8
latent_coef = 0.5
drop_dt = 0.25

MESH = pl.DeviceIdType.MESH
LANES = 128
SUB = 8
SLOTS = 2
ROWS = 3 * SLOTS
F32 = jnp.float32
BF16 = jnp.bfloat16


def split3(value):
    high = value.astype(BF16)
    rest = value - high.astype(F32)
    middle = rest.astype(BF16)
    low = (rest - middle.astype(F32)).astype(BF16)
    return high, middle, low


def softplus(x):
    return jnp.maximum(x, 0.0) + jnp.log1p(jnp.exp(-jnp.abs(x)))


def droplet_step(mass_now, temp_now, fuel_gas, temp_gas):
    src_mass = jnp.zeros_like(mass_now)
    src_energy = jnp.zeros_like(mass_now)
    for substep in range(SUBSTEPS):
        evap_rate = evap_coef * softplus(temp_now - fuel_gas)
        heat_flow = heat_coef * (temp_gas - temp_now)
        shrunk = mass_now * jnp.exp(-drop_dt * evap_rate)
        src_mass = src_mass + (mass_now - shrunk)
        src_energy = src_energy - drop_dt * heat_flow * mass_now
        temp_now = temp_now + drop_dt * (heat_flow - latent_coef * evap_rate)
        mass_now = shrunk
    return mass_now, temp_now, src_mass, src_energy


def kernel(
    n_gx, side,
    gas_hbm, kappa_hbm, vel_hbm, mass_hbm, temp_hbm, fill_hbm, cell_hbm, dest_hbm,
    gas_out, mass_out, temp_out,
    gas, kappa, vel, mass, temp, fill, cell, dest, dest_s,
    tables, outgo, relay, arrive, halo_x, halo_y, own_gas,
    in_sem, ready_z, ready_x, ready_d,
    gp_send, dp_send, g1_send, g1_recv, d1_send, d1_recv, g2_send, g2_recv, d2_send, d2_recv, halo_send, halo_recv,
):
    n_yz = side * side
    gx = lax.axis_index("gx")
    me = lax.axis_index("yz")
    me_x, me_z = me // side, me % side
    nfield = gas.shape[0]
    blocks = mass.shape[0]
    half = SUB // 2
    has_xm, has_xp = gx > 0, gx < n_gx - 1
    has_ym, has_yp = me > 0, me < n_yz - 1
    wrap_up = jnp.logical_and(me_z == side - 1, has_yp)
    wrap_down = jnp.logical_and(me_z == 0, has_ym)

    one = jnp.int32(1)
    zero = jnp.int32(0)

    late_z = jnp.where(jnp.logical_and(gx == 0, me_x == 0), one, zero)
    late_x = jnp.where(jnp.logical_and(gx == 0, me_z == 0), one, zero)
    is_late = jnp.logical_and(gx == 0, me == 0)
    past_corner = jnp.logical_and(jnp.logical_and(gx == 0, me_x == 0), me_z > 0)
    by_corner = jnp.logical_and(jnp.logical_and(gx == 0, me_z == 0), me_x > 0)

    def rank_z(z):
        late = jnp.where(z == 0, side - 2, jnp.where(z == side - 1, side - 1, z - 1))
        return jnp.where(late_z == 1, late, z)

    def turn_z(t):
        late = jnp.where(t == side - 2, 0, jnp.where(t == side - 1, side - 1, t + 1))
        return jnp.where(is_late, t, jnp.where(late_z == 1, late, t))

    def rank_x(x):
        return (jnp.where(x < side // 2, x, side // 2 + side - 1 - x) + side - late_x) % side

    my_rank = rank_x(me_x)
    my_turn = rank_z(me_z)

    def signal(sem, where):
        pl.semaphore_signal(sem, inc=1, device_id=where, device_id_type=MESH)

    loads = [
        pltpu.make_async_copy(src, dst, in_sem.at[i])
        for i, (src, dst) in enumerate(
            (
                (gas_hbm.at[0], tables.at[me_z, me_x, 0]),
                (gas_hbm.at[nfield - 1], tables.at[me_z, me_x, 1]),
                (dest_hbm, dest), (fill_hbm, fill), (cell_hbm, cell), (mass_hbm, mass),
                (temp_hbm, temp), (dest_hbm, dest_s),
                (gas_hbm, gas), (kappa_hbm, kappa), (vel_hbm, vel),
            )
        )
    ]
    for load in loads:
        load.start()

    halo_x[...] = jnp.zeros_like(halo_x)
    halo_y[...] = jnp.zeros_like(halo_y)

    barrier = pltpu.get_barrier_semaphore()

    def greet_z(z, carry):
        @pl.when(rank_z(z) > my_turn)
        def _():
            signal(barrier, {"yz": me_x * side + z})

        return carry

    def greet_x(x, carry):
        @pl.when(rank_x(x) > my_rank)
        def _():
            signal(barrier, {"yz": x * side + me_z})

        return carry

    lax.fori_loop(0, side, greet_z, 0)
    lax.fori_loop(0, side, greet_x, 0)

    @pl.when(by_corner)
    def _():
        def greet(z, carry):
            signal(barrier, {"yz": z})
            return carry

        lax.fori_loop(1, side, greet, 0)

    @pl.when(has_xm)
    def _():
        signal(barrier, {"gx": gx - 1})

    @pl.when(has_xp)
    def _():
        signal(barrier, {"gx": gx + 1})

    @pl.when(wrap_down)
    def _():
        signal(barrier, {"yz": me - 1})

    pl.semaphore_wait(
        barrier,
        my_turn + my_rank + jnp.where(has_xm, one, zero) + jnp.where(has_xp, one, zero)
        + jnp.where(wrap_up, one, zero) + jnp.where(past_corner, side - 1, 0),
    )
    for load in loads[:2]:
        load.wait()

    def remote(src, dst, send_sem, recv_sem, where):
        return pltpu.make_async_remote_copy(
            src_ref=src, dst_ref=dst, send_sem=send_sem, recv_sem=recv_sem,
            device_id=where, device_id_type=MESH,
        )

    def kinds(z):
        return pl.ds(z * ROWS, ROWS)

    def gas_along_z(z):
        mine = tables.at[me_z, me_x]
        return remote(mine, mine, g1_send, g1_recv.at[me_z], {"yz": me_x * side + z})

    def drops_along_z(z):
        return remote(outgo.at[kinds(z)], relay.at[kinds(me_z)], d1_send, d1_recv.at[me_z], {"yz": me_x * side + z})

    def gas_along_x(z, x):
        tile = tables.at[z, me_x]
        return remote(tile, tile, g2_send, g2_recv.at[z], {"yz": x * side + me_z})

    def drops_along_x(z, x):
        return remote(
            relay.at[kinds(z), x], arrive.at[kinds(z), me_x],
            d2_send, d2_recv.at[z], {"yz": x * side + me_z},
        )

    def early_gas(z, carry):
        @pl.when(rank_z(z) < my_turn)
        def _():
            gas_along_z(z).start()

        return carry

    lax.fori_loop(0, side, early_gas, 0)

    def gas_past(x):
        tile = tables.at[me_z, me_x]
        return remote(tile, tile, gp_send, g2_recv.at[me_z], {"yz": x * side})

    def drops_past(x):
        return remote(
            outgo.at[kinds(0), x], arrive.at[kinds(me_z), me_x], dp_send, d2_recv.at[me_z], {"yz": x * side}
        )

    def past(make):
        @pl.when(past_corner)
        def _():
            def send(x, carry):
                make(x).start()
                return carry

            lax.fori_loop(1, side, send, 0)

    past(gas_past)

    def tell_z(z, carry):
        @pl.when(rank_z(z) < my_turn)
        def _():
            signal(ready_z.at[me_z], {"yz": me_x * side + z})

        return carry

    def tell_x(x, carry):
        @pl.when(rank_x(x) < my_rank)
        def _():
            signal(ready_x.at[me_x], {"yz": x * side + me_z})

        return carry

    lax.fori_loop(0, side, tell_z, 0)
    lax.fori_loop(0, side, tell_x, 0)

    @pl.when(wrap_up)
    def _():
        signal(ready_d, {"yz": me + 1})


    for load in loads[2:8]:
        load.wait()
    row_i = lax.broadcasted_iota(jnp.int32, (blocks, blocks), 0)
    col_i = lax.broadcasted_iota(jnp.int32, (blocks, blocks), 1)
    dest_row = jnp.broadcast_to(dest[...], (blocks, blocks)).astype(F32)
    fill_row = jnp.broadcast_to(fill[...], (blocks, blocks)).astype(F32)
    dest_col = jnp.sum(jnp.where(row_i == col_i, dest_row, 0.0), axis=1, keepdims=True)
    fill_col = jnp.sum(jnp.where(row_i == col_i, fill_row, 0.0), axis=1, keepdims=True)
    same = jnp.where(dest_row == dest_col, 1.0, 0.0)
    rank_row = jnp.sum(jnp.where(row_i < col_i, same, 0.0), axis=0, keepdims=True)
    swapped_dest = (dest[...] % side) * side + dest[...] // side
    slot_row = rank_row * n_yz + swapped_dest.astype(F32)
    total = SLOTS * n_yz
    pick_slot = jnp.where(
        lax.broadcasted_iota(jnp.int32, (total, blocks), 0).astype(F32) == slot_row, 1.0, 0.0
    ).astype(BF16)
    lane = lax.broadcasted_iota(jnp.int32, (blocks, LANES), 1).astype(F32)
    living = lane < fill_col
    code = jnp.where(living, cell[...] + 1, 0).astype(F32)
    packed = jnp.concatenate([mass[...], temp[...], code], axis=1)
    placed = sum(
        jnp.dot(pick_slot, part, preferred_element_type=F32) for part in split3(packed)
    )
    for kind in range(3):
        for slot in range(SLOTS):
            for z in range(side):
                start = slot * n_yz + z * side
                outgo[z * ROWS + kind * SLOTS + slot] = placed[
                    start : start + side, kind * LANES : (kind + 1) * LANES
                ]

    def early_drops(z, carry):
        @pl.when(rank_z(z) < my_turn)
        def _():
            drops_along_z(z).start()

        return carry

    lax.fori_loop(0, side, early_drops, 0)
    past(drops_past)

    for load in loads[8:]:
        load.wait()

    def halo_copy(src, dst, index, where):
        return remote(src, dst, halo_send.at[index], halo_recv.at[index], where)

    to_xp = [halo_copy(gas.at[:, half:SUB], halo_x.at[:, 0:half], 0, {"gx": gx + 1})]
    to_xm = [halo_copy(gas.at[:, 0:half], halo_x.at[:, half:SUB], 1, {"gx": gx - 1})]
    to_yp = [
        halo_copy(gas.at[:, pl.ds(g + half - 1, 1)], halo_y.at[:, pl.ds(g, 1)], 2 + i, {"yz": me + 1})
        for i, g in enumerate((0, half))
    ]
    to_ym = [
        halo_copy(gas.at[:, pl.ds(g, 1)], halo_y.at[:, pl.ds(g + half - 1, 1)], 4 + i, {"yz": me - 1})
        for i, g in enumerate((0, half))
    ]

    def start_if(condition, copies):
        @pl.when(condition)
        def _():
            for copy in copies:
                copy.start()

    start_if(has_xp, to_xp)
    start_if(has_xm, to_xm)
    start_if(wrap_up, to_yp)
    up_z, down_z = me_z < side - 1, me_z > 0
    start_if(jnp.logical_and(up_z, rank_z(me_z + 1) < my_turn), to_yp)
    start_if(jnp.logical_and(down_z, rank_z(me_z - 1) < my_turn), to_ym)
    relay[kinds(me_z)] = outgo[kinds(me_z)]

    def await_x(x, carry):
        @pl.when(jnp.logical_and(rank_x(x) > my_rank, jnp.logical_not(jnp.logical_and(by_corner, x == 0))))
        def _():
            pl.semaphore_wait(ready_x.at[x], 1)

        return carry

    lax.fori_loop(0, side, await_x, 0)

    def step_on(z):
        @pl.when(rank_z(z) > my_turn)
        def _():
            pl.semaphore_wait(ready_z.at[z], 1)
            gas_along_z(z).start()
            drops_along_z(z).start()

        start_if(jnp.logical_and(z == me_z + 1, rank_z(z) > my_turn), to_yp)
        start_if(jnp.logical_and(z == me_z - 1, rank_z(z) > my_turn), to_ym)

        @pl.when(z != me_z)
        def _():
            remote(
                tables.at[z, me_x], tables.at[z, me_x], g1_send, g1_recv.at[z], {"yz": me}
            ).wait_recv()

        relays = jnp.logical_or(jnp.logical_not(is_late), z == me_z)
        first = jnp.where(by_corner, one, zero)

        def forward_gas(x, carry):
            @pl.when(jnp.logical_and(x != me_x, relays))
            def _():
                gas_along_x(z, x).start()

            return carry

        lax.fori_loop(first, side, forward_gas, 0)

        @pl.when(z != me_z)
        def _():
            remote(relay.at[kinds(z)], relay.at[kinds(z)], d1_send, d1_recv.at[z], {"yz": me}).wait_recv()

        def forward_drops(x, carry):
            @pl.when(jnp.logical_and(x != me_x, relays))
            def _():
                drops_along_x(z, x).start()

            return carry

        lax.fori_loop(first, side, forward_drops, 0)
        arrive[kinds(z), pl.ds(me_x, 1), :] = relay[kinds(z), pl.ds(me_x, 1), :]

    def bulk(view, sem):
        return pltpu.make_async_copy(view, view, sem)

    row_ids = lax.broadcasted_iota(jnp.int32, (LANES, LANES), 0)
    up_rows = lax.broadcasted_iota(jnp.int32, (SUB, LANES), 0)

    def group_in(z):
        bulk(arrive.at[kinds(z), pl.ds(0, side - 1)], d2_recv.at[z]).wait()

        def kind_of(kind):
            return jnp.concatenate(
                [
                    arrive[z * ROWS + kind * SLOTS + slot]
                    for slot in range(SLOTS)
                ],
                axis=0,
            )

        mass_in, temp_in = kind_of(0), kind_of(1)
        place = kind_of(2).astype(jnp.int32) - 1
        lower = place & (LANES - 1)
        upper = place >> 7
        fuel_gas = jnp.zeros_like(mass_in)
        temp_gas = jnp.zeros_like(mass_in)
        fuel_field = tables[me_z, me_x, 0]
        temp_field = tables[me_z, me_x, 1]
        for u in range(SUB):
            here = upper == u
            fuel_row = jnp.broadcast_to(fuel_field[u : u + 1], mass_in.shape)
            temp_row = jnp.broadcast_to(temp_field[u : u + 1], mass_in.shape)
            fuel_gas = jnp.where(
                here, jnp.take_along_axis(fuel_row, lower, axis=1, mode="promise_in_bounds"), fuel_gas
            )
            temp_gas = jnp.where(
                here, jnp.take_along_axis(temp_row, lower, axis=1, mode="promise_in_bounds"), temp_gas
            )
        return mass_in, temp_in, fuel_gas, temp_gas, lower, upper

    def deposit(lower, upper, src_mass, src_energy):
        values = []
        for value in (src_mass, src_energy):
            high = value.astype(BF16).astype(F32)
            values += [high, value - high]
        hots, weighted = [], []
        for b in range(lower.shape[0]):
            hots.append(jnp.where(lower[b : b + 1] == row_ids, 1.0, 0.0).astype(BF16))
            here = upper[b : b + 1] == up_rows
            weighted.append(
                jnp.concatenate([jnp.where(here, v[b : b + 1], 0.0) for v in values], axis=0).astype(BF16)
            )
        return lax.dot_general(
            jnp.concatenate(weighted, axis=1), jnp.concatenate(hots, axis=1),
            (((1,), (1,)), ((), ())), preferred_element_type=F32,
        )

    def group(z):
        mass_in, temp_in, fuel_gas, temp_gas, lower, upper = group_in(z)
        _, _, src_mass, src_energy = droplet_step(mass_in, temp_in, fuel_gas, temp_gas)
        return deposit(lower, upper, src_mass, src_energy)

    def gas_ready(z):
        bulk(tables.at[z, pl.ds(0, side - 1)], g2_recv.at[z]).wait()

    def advance(t, carry):
        step_on(turn_z(t))
        return carry

    lax.fori_loop(0, side, advance, 0)

    summed = lax.fori_loop(
        0, side - 1, lambda z, summed: summed + group(z), jnp.zeros((4 * SUB, LANES), F32)
    )

    @pl.when(wrap_down)
    def _():
        pl.semaphore_wait(ready_d, 1)
        for copy in to_ym:
            copy.start()

    for exists, copies in ((has_xm, to_xp), (has_xp, to_xm), (has_ym, to_yp), (has_yp, to_ym)):

        @pl.when(exists)
        def _(copies=copies):
            for copy in copies:
                copy.wait_recv()

    sub_id = lax.broadcasted_iota(jnp.int32, (SUB, LANES), 0)
    lane_id = lax.broadcasted_iota(jnp.int32, (SUB, LANES), 1)
    first_x = sub_id < half
    first_y, last_y = sub_id % half == 0, sub_id % half == half - 1
    first_z, last_z = lane_id == 0, lane_id == LANES - 1
    kap, velo = kappa[...], vel[...]
    ends = {}
    for f in range(nfield):
        field, hx, hy = gas[f], halo_x[f], halo_y[f]
        swapped = pltpu.roll(field, half, 0)
        before_x = jnp.where(first_x, hx, swapped)
        after_x = jnp.where(first_x, swapped, hx)
        before_y = jnp.where(first_y, hy, pltpu.roll(field, 1, 0))
        after_y = jnp.where(last_y, hy, pltpu.roll(field, SUB - 1, 0))
        before_z = jnp.where(first_z, field, pltpu.roll(field, 1, 1))
        after_z = jnp.where(last_z, field, pltpu.roll(field, LANES - 1, 1))
        beside = after_x + before_x + after_y + before_y + after_z + before_z
        moved = field + kap * (beside - 6.0 * field) - velo * (field - before_x)
        if f in (0, nfield - 1):
            ends[f] = moved
        else:
            gas_out[f] = moved

    @pl.when(by_corner)
    def _():
        pl.semaphore_wait(ready_x.at[0], 1)

        def forward(z, carry):
            gas_along_x(z, 0).start()
            drops_along_x(z, 0).start()
            return carry

        lax.fori_loop(0, side, forward, 0)

    for z in range(side):
        gas_ready(z)
    for j in range(blocks):
        target = dest_s[0, j]
        z, x = target % side, target // side
        place = cell[pl.ds(j, 1), :]
        lower = jnp.broadcast_to(place & (LANES - 1), (SUB, LANES))
        here = (place >> 7) == up_rows
        for kind in range(2):
            looked = jnp.take_along_axis(tables[z, x, kind], lower, axis=1, mode="promise_in_bounds")
            own_gas[kind, pl.ds(j, 1), :] = jnp.sum(jnp.where(here, looked, 0.0), axis=0, keepdims=True)
    mass_in, temp_in, fuel_gas, temp_gas, lower, upper = group_in(side - 1)
    _, _, src_mass, src_energy = droplet_step(mass_in, temp_in, fuel_gas, temp_gas)
    own_mass, own_temp, _, _ = droplet_step(mass[...], temp[...], own_gas[0], own_gas[1])
    mass_out[...] = jnp.where(living, own_mass, 0.0)
    temp_out[...] = jnp.where(living, own_temp, 0.0)
    summed = summed + deposit(lower, upper, src_mass, src_energy)
    gas_out[0] = ends[0] + (summed[0:SUB] + summed[SUB : 2 * SUB])
    gas_out[nfield - 1] = ends[nfield - 1] + (summed[2 * SUB : 3 * SUB] + summed[3 * SUB : 4 * SUB])

    bulk(tables.at[0, pl.ds(0, side - 1)], g1_send).wait()
    bulk(outgo.at[pl.ds(0, (side - 1) * ROWS)], d1_send).wait()

    @pl.when(is_late)
    def _():
        bulk(tables.at[0, pl.ds(0, side - 1)], g2_send).wait()
        bulk(arrive.at[kinds(0), pl.ds(0, side - 1)], d2_send).wait()

    @pl.when(jnp.logical_not(is_late))
    def _():
        bulk(tables.at[pl.ds(0, side - 1)], g2_send).wait()
        bulk(arrive.at[:, pl.ds(0, side - 1)], d2_send).wait()

    @pl.when(past_corner)
    def _():
        bulk(tables.at[0, pl.ds(0, side - 1)], gp_send).wait()
        bulk(arrive.at[kinds(0), pl.ds(0, side - 1)], dp_send).wait()

    for exists, copies in ((has_xp, to_xp), (has_xm, to_xm), (has_yp, to_yp), (has_ym, to_ym)):

        @pl.when(exists)
        def _(copies=copies):
            for copy in copies:
                copy.wait_send()


def solution(mesh):
    n_gx, n_yz = mesh.shape["gx"], mesh.shape["yz"]
    side = math.isqrt(n_yz)
    assert side * side == n_yz

    def body(gas, kappa, velocity, drop_mass, drop_temp, block_fill, drop_cell, block_dest):
        nfield, cx, cy, cz = gas.shape
        blocks = drop_mass.shape[0]
        any_spec = pl.BlockSpec(memory_space=pl.ANY)
        vmem_spec = pl.BlockSpec(memory_space=pltpu.VMEM)
        tile = (cx * cy, cz)
        dma = pltpu.SemaphoreType.DMA
        regular = pltpu.SemaphoreType.REGULAR
        gas_next, mass_next, temp_next = pl.pallas_call(
            functools.partial(kernel, n_gx, side),
            out_shape=(
                pltpu.VMEM((nfield,) + tile, F32),
                pltpu.VMEM(drop_mass.shape, F32),
                pltpu.VMEM(drop_mass.shape, F32),
            ),
            in_specs=[any_spec] * 8,
            out_specs=(vmem_spec,) * 3,
            scratch_shapes=[
                pltpu.VMEM((nfield,) + tile, F32),
                pltpu.VMEM(tile, F32),
                pltpu.VMEM(tile, F32),
                pltpu.VMEM((blocks, LANES), F32),
                pltpu.VMEM((blocks, LANES), F32),
                pltpu.VMEM((1, blocks), jnp.int32),
                pltpu.VMEM((blocks, LANES), jnp.int32),
                pltpu.VMEM((1, blocks), jnp.int32),
                pltpu.SMEM((1, blocks), jnp.int32),
                pltpu.VMEM((side, side, 2) + tile, F32),
                pltpu.VMEM((side * ROWS, side, LANES), F32),
                pltpu.VMEM((side * ROWS, side, LANES), F32),
                pltpu.VMEM((side * ROWS, side, LANES), F32),
                pltpu.VMEM((nfield,) + tile, F32),
                pltpu.VMEM((nfield,) + tile, F32),
                pltpu.VMEM((2, blocks, LANES), F32),
                dma((11,)),
                regular((side,)),
                regular((side,)),
                regular,
                dma, dma,
                dma, dma((side,)), dma, dma((side,)),
                dma, dma((side,)), dma, dma((side,)),
                dma((6,)), dma((6,)),
            ],
            compiler_params=pltpu.CompilerParams(collective_id=0, has_side_effects=True),
            name="spray_step",
        )(
            gas.reshape((nfield,) + tile),
            kappa.reshape(tile),
            velocity.reshape(tile),
            drop_mass,
            drop_temp,
            block_fill.reshape(1, blocks),
            drop_cell,
            block_dest.reshape(1, blocks),
        )
        return gas_next.reshape(gas.shape), mass_next, temp_next

    in_specs = (
        P(None, "gx", "yz", None),
        P("gx", "yz", None),
        P("gx", "yz", None),
        P(("gx", "yz"), None),
        P(("gx", "yz"), None),
        P(("gx", "yz")),
        P(("gx", "yz"), None),
        P(("gx", "yz"), None),
    )
    out_specs = (P(None, "gx", "yz", None), P(("gx", "yz"), None), P(("gx", "yz"), None))
    return jax.shard_map(body, mesh=mesh, in_specs=in_specs, out_specs=out_specs, check_vma=False)
```

```python
import functools
import math

import jax
import jax.numpy as jnp
from jax import lax
from jax.experimental import pallas as pl
from jax.experimental.pallas import tpu as pltpu
from jax.sharding import PartitionSpec as P

SUBSTEPS = 4
evap_coef = 0.3
heat_coef = 0.8
latent_coef = 0.5
drop_dt = 0.25

MESH = pl.DeviceIdType.MESH
LANES = 128
SUB = 8
SLOTS = 2
ROWS = 3 * SLOTS
F32 = jnp.float32
BF16 = jnp.bfloat16


def split3(value):
    high = value.astype(BF16)
    rest = value - high.astype(F32)
    middle = rest.astype(BF16)
    low = (rest - middle.astype(F32)).astype(BF16)
    return high, middle, low


def softplus(x):
    return jnp.maximum(x, 0.0) + jnp.log1p(jnp.exp(-jnp.abs(x)))


def droplet_step(mass_now, temp_now, fuel_gas, temp_gas):
    src_mass = jnp.zeros_like(mass_now)
    src_energy = jnp.zeros_like(mass_now)
    for substep in range(SUBSTEPS):
        evap_rate = evap_coef * softplus(temp_now - fuel_gas)
        heat_flow = heat_coef * (temp_gas - temp_now)
        shrunk = mass_now * jnp.exp(-drop_dt * evap_rate)
        src_mass = src_mass + (mass_now - shrunk)
        src_energy = src_energy - drop_dt * heat_flow * mass_now
        temp_now = temp_now + drop_dt * (heat_flow - latent_coef * evap_rate)
        mass_now = shrunk
    return mass_now, temp_now, src_mass, src_energy


def kernel(
    n_gx, side,
    gas_hbm, kappa_hbm, vel_hbm, mass_hbm, temp_hbm, fill_hbm, cell_hbm, dest_hbm,
    gas_out, mass_out, temp_out,
    gas, kappa, vel, mass, temp, fill, cell, dest, dest_s,
    tables, outgo, relay, arrive, halo_x, halo_y, picked,
    in_sem, ready_z, ready_x, ready_d,
    gp_send, dp_send, g1_send, g1_recv, d1_send, d1_recv, g2_send, g2_recv, d2_send, d2_recv, halo_send, halo_recv,
):
    n_yz = side * side
    gx = lax.axis_index("gx")
    me = lax.axis_index("yz")
    me_x, me_z = me // side, me % side
    nfield = gas.shape[0]
    blocks = mass.shape[0]
    half = SUB // 2
    has_xm, has_xp = gx > 0, gx < n_gx - 1
    has_ym, has_yp = me > 0, me < n_yz - 1
    wrap_up = jnp.logical_and(me_z == side - 1, has_yp)
    wrap_down = jnp.logical_and(me_z == 0, has_ym)

    one = jnp.int32(1)
    zero = jnp.int32(0)

    late_z = jnp.where(jnp.logical_and(gx == 0, me_x == 0), one, zero)
    late_x = jnp.where(jnp.logical_and(gx == 0, me_z == 0), one, zero)
    is_late = jnp.logical_and(gx == 0, me == 0)
    past_corner = jnp.logical_and(jnp.logical_and(gx == 0, me_x == 0), me_z > 0)
    by_corner = jnp.logical_and(jnp.logical_and(gx == 0, me_z == 0), me_x > 0)

    def rank_z(z):
        late = jnp.where(z == 0, side - 2, jnp.where(z == side - 1, side - 1, z - 1))
        return jnp.where(late_z == 1, late, z)

    def turn_z(t):
        late = jnp.where(t == side - 2, 0, jnp.where(t == side - 1, side - 1, t + 1))
        return jnp.where(is_late, t, jnp.where(late_z == 1, late, t))

    def rank_x(x):
        return (jnp.where(x < side // 2, x, side // 2 + side - 1 - x) + side - late_x) % side

    my_rank = rank_x(me_x)
    my_turn = rank_z(me_z)

    def signal(sem, where):
        pl.semaphore_signal(sem, inc=1, device_id=where, device_id_type=MESH)

    loads = [
        pltpu.make_async_copy(src, dst, in_sem.at[i])
        for i, (src, dst) in enumerate(
            (
                (gas_hbm.at[0], tables.at[me_z, me_x, 0]),
                (gas_hbm.at[nfield - 1], tables.at[me_z, me_x, 1]),
                (dest_hbm, dest), (fill_hbm, fill), (cell_hbm, cell), (mass_hbm, mass),
                (temp_hbm, temp), (dest_hbm, dest_s),
                (gas_hbm, gas), (kappa_hbm, kappa), (vel_hbm, vel),
            )
        )
    ]
    for load in loads:
        load.start()

    halo_x[...] = jnp.zeros_like(halo_x)
    halo_y[...] = jnp.zeros_like(halo_y)

    barrier = pltpu.get_barrier_semaphore()

    def greet_z(z, carry):
        @pl.when(rank_z(z) > my_turn)
        def _():
            signal(barrier, {"yz": me_x * side + z})

        return carry

    def greet_x(x, carry):
        @pl.when(rank_x(x) > my_rank)
        def _():
            signal(barrier, {"yz": x * side + me_z})

        return carry

    lax.fori_loop(0, side, greet_z, 0)
    lax.fori_loop(0, side, greet_x, 0)

    @pl.when(by_corner)
    def _():
        def greet(z, carry):
            signal(barrier, {"yz": z})
            return carry

        lax.fori_loop(1, side, greet, 0)

    @pl.when(has_xm)
    def _():
        signal(barrier, {"gx": gx - 1})

    @pl.when(has_xp)
    def _():
        signal(barrier, {"gx": gx + 1})

    @pl.when(wrap_down)
    def _():
        signal(barrier, {"yz": me - 1})

    pl.semaphore_wait(
        barrier,
        my_turn + my_rank + jnp.where(has_xm, one, zero) + jnp.where(has_xp, one, zero)
        + jnp.where(wrap_up, one, zero) + jnp.where(past_corner, side - 1, 0),
    )
    for load in loads[:2]:
        load.wait()

    def remote(src, dst, send_sem, recv_sem, where):
        return pltpu.make_async_remote_copy(
            src_ref=src, dst_ref=dst, send_sem=send_sem, recv_sem=recv_sem,
            device_id=where, device_id_type=MESH,
        )

    def kinds(z):
        return pl.ds(z * ROWS, ROWS)

    def gas_along_z(z):
        mine = tables.at[me_z, me_x]
        return remote(mine, mine, g1_send, g1_recv.at[me_z], {"yz": me_x * side + z})

    def drops_along_z(z):
        return remote(outgo.at[kinds(z)], relay.at[kinds(me_z)], d1_send, d1_recv.at[me_z], {"yz": me_x * side + z})

    def gas_along_x(z, x):
        tile = tables.at[z, me_x]
        return remote(tile, tile, g2_send, g2_recv.at[z], {"yz": x * side + me_z})

    def drops_along_x(z, x):
        return remote(
            relay.at[kinds(z), x], arrive.at[kinds(z), me_x],
            d2_send, d2_recv.at[z], {"yz": x * side + me_z},
        )

    def early_gas(z, carry):
        @pl.when(rank_z(z) < my_turn)
        def _():
            gas_along_z(z).start()

        return carry

    lax.fori_loop(0, side, early_gas, 0)

    def gas_past(x):
        tile = tables.at[me_z, me_x]
        return remote(tile, tile, gp_send, g2_recv.at[me_z], {"yz": x * side})

    def drops_past(x):
        return remote(
            outgo.at[kinds(0), x], arrive.at[kinds(me_z), me_x], dp_send, d2_recv.at[me_z], {"yz": x * side}
        )

    def past(make):
        @pl.when(past_corner)
        def _():
            def send(x, carry):
                make(x).start()
                return carry

            lax.fori_loop(1, side, send, 0)

    past(gas_past)

    def tell_z(z, carry):
        @pl.when(rank_z(z) < my_turn)
        def _():
            signal(ready_z.at[me_z], {"yz": me_x * side + z})

        return carry

    def tell_x(x, carry):
        @pl.when(rank_x(x) < my_rank)
        def _():
            signal(ready_x.at[me_x], {"yz": x * side + me_z})

        return carry

    lax.fori_loop(0, side, tell_z, 0)
    lax.fori_loop(0, side, tell_x, 0)

    @pl.when(wrap_up)
    def _():
        signal(ready_d, {"yz": me + 1})


    for load in loads[2:8]:
        load.wait()
    row_i = lax.broadcasted_iota(jnp.int32, (blocks, blocks), 0)
    col_i = lax.broadcasted_iota(jnp.int32, (blocks, blocks), 1)
    dest_row = jnp.broadcast_to(dest[...], (blocks, blocks)).astype(F32)
    fill_row = jnp.broadcast_to(fill[...], (blocks, blocks)).astype(F32)
    dest_col = jnp.sum(jnp.where(row_i == col_i, dest_row, 0.0), axis=1, keepdims=True)
    fill_col = jnp.sum(jnp.where(row_i == col_i, fill_row, 0.0), axis=1, keepdims=True)
    same = jnp.where(dest_row == dest_col, 1.0, 0.0)
    rank_row = jnp.sum(jnp.where(row_i < col_i, same, 0.0), axis=0, keepdims=True)
    swapped_dest = (dest[...] % side) * side + dest[...] // side
    slot_row = rank_row * n_yz + swapped_dest.astype(F32)
    total = SLOTS * n_yz
    pick_slot = jnp.where(
        lax.broadcasted_iota(jnp.int32, (total, blocks), 0).astype(F32) == slot_row, 1.0, 0.0
    ).astype(BF16)
    lane = lax.broadcasted_iota(jnp.int32, (blocks, LANES), 1).astype(F32)
    living = lane < fill_col
    code = jnp.where(living, cell[...] + 1, 0).astype(F32)
    packed = jnp.concatenate([mass[...], temp[...], code], axis=1)
    placed = sum(
        jnp.dot(pick_slot, part, preferred_element_type=F32) for part in split3(packed)
    )
    for kind in range(3):
        for slot in range(SLOTS):
            for z in range(side):
                start = slot * n_yz + z * side
                outgo[z * ROWS + kind * SLOTS + slot] = placed[
                    start : start + side, kind * LANES : (kind + 1) * LANES
                ]

    def early_drops(z, carry):
        @pl.when(rank_z(z) < my_turn)
        def _():
            drops_along_z(z).start()

        return carry

    lax.fori_loop(0, side, early_drops, 0)
    past(drops_past)

    for load in loads[8:]:
        load.wait()

    def halo_copy(src, dst, index, where):
        return remote(src, dst, halo_send.at[index], halo_recv.at[index], where)

    to_xp = [halo_copy(gas.at[:, half:SUB], halo_x.at[:, 0:half], 0, {"gx": gx + 1})]
    to_xm = [halo_copy(gas.at[:, 0:half], halo_x.at[:, half:SUB], 1, {"gx": gx - 1})]
    to_yp = [
        halo_copy(gas.at[:, pl.ds(g + half - 1, 1)], halo_y.at[:, pl.ds(g, 1)], 2 + i, {"yz": me + 1})
        for i, g in enumerate((0, half))
    ]
    to_ym = [
        halo_copy(gas.at[:, pl.ds(g, 1)], halo_y.at[:, pl.ds(g + half - 1, 1)], 4 + i, {"yz": me - 1})
        for i, g in enumerate((0, half))
    ]

    def start_if(condition, copies):
        @pl.when(condition)
        def _():
            for copy in copies:
                copy.start()

    start_if(has_xp, to_xp)
    start_if(has_xm, to_xm)
    start_if(wrap_up, to_yp)
    up_z, down_z = me_z < side - 1, me_z > 0
    start_if(jnp.logical_and(up_z, rank_z(me_z + 1) < my_turn), to_yp)
    start_if(jnp.logical_and(down_z, rank_z(me_z - 1) < my_turn), to_ym)
    relay[kinds(me_z)] = outgo[kinds(me_z)]

    def await_x(x, carry):
        @pl.when(jnp.logical_and(rank_x(x) > my_rank, jnp.logical_not(jnp.logical_and(by_corner, x == 0))))
        def _():
            pl.semaphore_wait(ready_x.at[x], 1)

        return carry

    lax.fori_loop(0, side, await_x, 0)

    def step_on(z):
        @pl.when(rank_z(z) > my_turn)
        def _():
            pl.semaphore_wait(ready_z.at[z], 1)
            gas_along_z(z).start()
            drops_along_z(z).start()

        start_if(jnp.logical_and(z == me_z + 1, rank_z(z) > my_turn), to_yp)
        start_if(jnp.logical_and(z == me_z - 1, rank_z(z) > my_turn), to_ym)

        @pl.when(z != me_z)
        def _():
            remote(
                tables.at[z, me_x], tables.at[z, me_x], g1_send, g1_recv.at[z], {"yz": me}
            ).wait_recv()

        relays = jnp.logical_or(jnp.logical_not(is_late), z == me_z)
        first = jnp.where(by_corner, one, zero)

        def forward_gas(x, carry):
            @pl.when(jnp.logical_and(x != me_x, relays))
            def _():
                gas_along_x(z, x).start()

            return carry

        lax.fori_loop(first, side, forward_gas, 0)

        @pl.when(z != me_z)
        def _():
            remote(relay.at[kinds(z)], relay.at[kinds(z)], d1_send, d1_recv.at[z], {"yz": me}).wait_recv()

        def forward_drops(x, carry):
            @pl.when(jnp.logical_and(x != me_x, relays))
            def _():
                drops_along_x(z, x).start()

            return carry

        lax.fori_loop(first, side, forward_drops, 0)
        arrive[kinds(z), pl.ds(me_x, 1), :] = relay[kinds(z), pl.ds(me_x, 1), :]

    def bulk(view, sem):
        return pltpu.make_async_copy(view, view, sem)

    row_ids = lax.broadcasted_iota(jnp.int32, (LANES, LANES), 0)
    up_rows = lax.broadcasted_iota(jnp.int32, (SUB, LANES), 0)

    def group_in(z):
        bulk(arrive.at[kinds(z), pl.ds(0, side - 1)], d2_recv.at[z]).wait()

        def kind_of(kind):
            return jnp.concatenate(
                [
                    arrive[z * ROWS + kind * SLOTS + slot]
                    for slot in range(SLOTS)
                ],
                axis=0,
            )

        mass_in, temp_in = kind_of(0), kind_of(1)
        place = kind_of(2).astype(jnp.int32) - 1
        lower = place & (LANES - 1)
        upper = place >> 7
        fuel_gas = jnp.zeros_like(mass_in)
        temp_gas = jnp.zeros_like(mass_in)
        fuel_field = tables[me_z, me_x, 0]
        temp_field = tables[me_z, me_x, 1]
        for u in range(SUB):
            here = upper == u
            fuel_row = jnp.broadcast_to(fuel_field[u : u + 1], mass_in.shape)
            temp_row = jnp.broadcast_to(temp_field[u : u + 1], mass_in.shape)
            fuel_gas = jnp.where(
                here, jnp.take_along_axis(fuel_row, lower, axis=1, mode="promise_in_bounds"), fuel_gas
            )
            temp_gas = jnp.where(
                here, jnp.take_along_axis(temp_row, lower, axis=1, mode="promise_in_bounds"), temp_gas
            )
        return mass_in, temp_in, fuel_gas, temp_gas, lower, upper

    def deposit(lower, upper, src_mass, src_energy):
        values = []
        for value in (src_mass, src_energy):
            high = value.astype(BF16).astype(F32)
            values += [high, value - high]
        hots, weighted = [], []
        for b in range(lower.shape[0]):
            hots.append(jnp.where(lower[b : b + 1] == row_ids, 1.0, 0.0).astype(BF16))
            here = upper[b : b + 1] == up_rows
            weighted.append(
                jnp.concatenate([jnp.where(here, v[b : b + 1], 0.0) for v in values], axis=0).astype(BF16)
            )
        return lax.dot_general(
            jnp.concatenate(weighted, axis=1), jnp.concatenate(hots, axis=1),
            (((1,), (1,)), ((), ())), preferred_element_type=F32,
        )

    def group(z):
        mass_in, temp_in, fuel_gas, temp_gas, lower, upper = group_in(z)
        _, _, src_mass, src_energy = droplet_step(mass_in, temp_in, fuel_gas, temp_gas)
        return deposit(lower, upper, src_mass, src_energy)

    def gas_ready(z):
        bulk(tables.at[z, pl.ds(0, side - 1)], g2_recv.at[z]).wait()

    def advance(t, carry):
        step_on(turn_z(t))
        return carry

    lax.fori_loop(0, side, advance, 0)

    summed = lax.fori_loop(
        0, side - 1, lambda z, summed: summed + group(z), jnp.zeros((4 * SUB, LANES), F32)
    )

    @pl.when(wrap_down)
    def _():
        pl.semaphore_wait(ready_d, 1)
        for copy in to_ym:
            copy.start()

    for exists, copies in ((has_xm, to_xp), (has_xp, to_xm), (has_ym, to_yp), (has_yp, to_ym)):

        @pl.when(exists)
        def _(copies=copies):
            for copy in copies:
                copy.wait_recv()

    sub_id = lax.broadcasted_iota(jnp.int32, (SUB, LANES), 0)
    lane_id = lax.broadcasted_iota(jnp.int32, (SUB, LANES), 1)
    first_x = sub_id < half
    first_y, last_y = sub_id % half == 0, sub_id % half == half - 1
    first_z, last_z = lane_id == 0, lane_id == LANES - 1
    kap, velo = kappa[...], vel[...]
    ends = {}
    for f in range(nfield):
        field, hx, hy = gas[f], halo_x[f], halo_y[f]
        swapped = pltpu.roll(field, half, 0)
        before_x = jnp.where(first_x, hx, swapped)
        after_x = jnp.where(first_x, swapped, hx)
        before_y = jnp.where(first_y, hy, pltpu.roll(field, 1, 0))
        after_y = jnp.where(last_y, hy, pltpu.roll(field, SUB - 1, 0))
        before_z = jnp.where(first_z, field, pltpu.roll(field, 1, 1))
        after_z = jnp.where(last_z, field, pltpu.roll(field, LANES - 1, 1))
        beside = after_x + before_x + after_y + before_y + after_z + before_z
        moved = field + kap * (beside - 6.0 * field) - velo * (field - before_x)
        if f in (0, nfield - 1):
            ends[f] = moved
        else:
            gas_out[f] = moved

    @pl.when(by_corner)
    def _():
        pl.semaphore_wait(ready_x.at[0], 1)

        def forward(z, carry):
            gas_along_x(z, 0).start()
            drops_along_x(z, 0).start()
            return carry

        lax.fori_loop(0, side, forward, 0)

    for z in range(side):
        gas_ready(z)
    for j in range(blocks):
        target = dest_s[0, j]
        z, x = target % side, target // side
        for kind in range(2):
            picked[kind, pl.ds(j * SUB, SUB), :] = tables[z, x, kind]
    own_lower = cell[...] & (LANES - 1)
    own_upper = cell[...] >> 7
    own_gas = []
    for kind in range(2):
        found = jnp.zeros((blocks, LANES), F32)
        for u in range(SUB):
            row = picked[kind, pl.ds(u, blocks, stride=SUB), :]
            looked = jnp.take_along_axis(row, own_lower, axis=1, mode="promise_in_bounds")
            found = jnp.where(own_upper == u, looked, found)
        own_gas.append(found)
    mass_in, temp_in, fuel_gas, temp_gas, lower, upper = group_in(side - 1)
    _, _, src_mass, src_energy = droplet_step(mass_in, temp_in, fuel_gas, temp_gas)
    own_mass, own_temp, _, _ = droplet_step(mass[...], temp[...], own_gas[0], own_gas[1])
    mass_out[...] = jnp.where(living, own_mass, 0.0)
    temp_out[...] = jnp.where(living, own_temp, 0.0)
    summed = summed + deposit(lower, upper, src_mass, src_energy)
    gas_out[0] = ends[0] + (summed[0:SUB] + summed[SUB : 2 * SUB])
    gas_out[nfield - 1] = ends[nfield - 1] + (summed[2 * SUB : 3 * SUB] + summed[3 * SUB : 4 * SUB])

    bulk(tables.at[0, pl.ds(0, side - 1)], g1_send).wait()
    bulk(outgo.at[pl.ds(0, (side - 1) * ROWS)], d1_send).wait()

    @pl.when(is_late)
    def _():
        bulk(tables.at[0, pl.ds(0, side - 1)], g2_send).wait()
        bulk(arrive.at[kinds(0), pl.ds(0, side - 1)], d2_send).wait()

    @pl.when(jnp.logical_not(is_late))
    def _():
        bulk(tables.at[pl.ds(0, side - 1)], g2_send).wait()
        bulk(arrive.at[:, pl.ds(0, side - 1)], d2_send).wait()

    @pl.when(past_corner)
    def _():
        bulk(tables.at[0, pl.ds(0, side - 1)], gp_send).wait()
        bulk(arrive.at[kinds(0), pl.ds(0, side - 1)], dp_send).wait()

    for exists, copies in ((has_xp, to_xp), (has_xm, to_xm), (has_yp, to_yp), (has_ym, to_ym)):

        @pl.when(exists)
        def _(copies=copies):
            for copy in copies:
                copy.wait_send()


def emit(gas_in, mass_in, temp_in, gas_out, mass_out, temp_out, sems):
    copies = [
        pltpu.make_async_copy(src, dst, sems.at[i])
        for i, (src, dst) in enumerate(((gas_in, gas_out), (mass_in, mass_out), (temp_in, temp_out)))
    ]
    for copy in copies:
        copy.start()
    for copy in copies:
        copy.wait()


def solution(mesh):
    n_gx, n_yz = mesh.shape["gx"], mesh.shape["yz"]
    side = math.isqrt(n_yz)
    assert side * side == n_yz

    def body(gas, kappa, velocity, drop_mass, drop_temp, block_fill, drop_cell, block_dest):
        nfield, cx, cy, cz = gas.shape
        blocks = drop_mass.shape[0]
        any_spec = pl.BlockSpec(memory_space=pl.ANY)
        vmem_spec = pl.BlockSpec(memory_space=pltpu.VMEM)
        tile = (cx * cy, cz)
        dma = pltpu.SemaphoreType.DMA
        regular = pltpu.SemaphoreType.REGULAR
        gas_next, mass_next, temp_next = pl.pallas_call(
            functools.partial(kernel, n_gx, side),
            out_shape=(
                pltpu.VMEM((nfield,) + tile, F32),
                pltpu.VMEM(drop_mass.shape, F32),
                pltpu.VMEM(drop_mass.shape, F32),
            ),
            in_specs=[any_spec] * 8,
            out_specs=(vmem_spec,) * 3,
            scratch_shapes=[
                pltpu.VMEM((nfield,) + tile, F32),
                pltpu.VMEM(tile, F32),
                pltpu.VMEM(tile, F32),
                pltpu.VMEM((blocks, LANES), F32),
                pltpu.VMEM((blocks, LANES), F32),
                pltpu.VMEM((1, blocks), jnp.int32),
                pltpu.VMEM((blocks, LANES), jnp.int32),
                pltpu.VMEM((1, blocks), jnp.int32),
                pltpu.SMEM((1, blocks), jnp.int32),
                pltpu.VMEM((side, side, 2) + tile, F32),
                pltpu.VMEM((side * ROWS, side, LANES), F32),
                pltpu.VMEM((side * ROWS, side, LANES), F32),
                pltpu.VMEM((side * ROWS, side, LANES), F32),
                pltpu.VMEM((nfield,) + tile, F32),
                pltpu.VMEM((nfield,) + tile, F32),
                pltpu.VMEM((2, blocks * SUB, LANES), F32),
                dma((11,)),
                regular((side,)),
                regular((side,)),
                regular,
                dma, dma,
                dma, dma((side,)), dma, dma((side,)),
                dma, dma((side,)), dma, dma((side,)),
                dma((6,)), dma((6,)),
            ],
            compiler_params=pltpu.CompilerParams(collective_id=0, has_side_effects=True),
            name="spray_step",
        )(
            gas.reshape((nfield,) + tile),
            kappa.reshape(tile),
            velocity.reshape(tile),
            drop_mass,
            drop_temp,
            block_fill.reshape(1, blocks),
            drop_cell,
            block_dest.reshape(1, blocks),
        )
        gas_next, mass_next, temp_next = pl.pallas_call(
            emit,
            out_shape=(
                jax.ShapeDtypeStruct((nfield,) + tile, F32),
                jax.ShapeDtypeStruct(drop_mass.shape, F32),
                jax.ShapeDtypeStruct(drop_mass.shape, F32),
            ),
            in_specs=(vmem_spec,) * 3,
            out_specs=(any_spec,) * 3,
            scratch_shapes=[dma((3,))],
            name="emit",
        )(*(pltpu.with_memory_space_constraint(a, pltpu.VMEM) for a in (gas_next, mass_next, temp_next)))
        return gas_next.reshape(gas.shape), mass_next, temp_next

    in_specs = (
        P(None, "gx", "yz", None),
        P("gx", "yz", None),
        P("gx", "yz", None),
        P(("gx", "yz"), None),
        P(("gx", "yz"), None),
        P(("gx", "yz")),
        P(("gx", "yz"), None),
        P(("gx", "yz"), None),
    )
    out_specs = (P(None, "gx", "yz", None), P(("gx", "yz"), None), P(("gx", "yz"), None))
    return jax.shard_map(body, mesh=mesh, in_specs=in_specs, out_specs=out_specs, check_vma=False)
```

```python
import functools
import math

import jax
import jax.numpy as jnp
from jax import lax
from jax.experimental import pallas as pl
from jax.experimental.pallas import tpu as pltpu
from jax.sharding import PartitionSpec as P

SUBSTEPS = 4
evap_coef = 0.3
heat_coef = 0.8
latent_coef = 0.5
drop_dt = 0.25

MESH = pl.DeviceIdType.MESH
LANES = 128
SUB = 8
SLOTS = 2
ROWS = 3 * SLOTS
F32 = jnp.float32
BF16 = jnp.bfloat16


def split3(value):
    high = value.astype(BF16)
    rest = value - high.astype(F32)
    middle = rest.astype(BF16)
    low = (rest - middle.astype(F32)).astype(BF16)
    return high, middle, low


def softplus(x):
    return jnp.maximum(x, 0.0) + jnp.log1p(jnp.exp(-jnp.abs(x)))


def droplet_step(mass_now, temp_now, fuel_gas, temp_gas):
    src_mass = jnp.zeros_like(mass_now)
    src_energy = jnp.zeros_like(mass_now)
    for substep in range(SUBSTEPS):
        evap_rate = evap_coef * softplus(temp_now - fuel_gas)
        heat_flow = heat_coef * (temp_gas - temp_now)
        shrunk = mass_now * jnp.exp(-drop_dt * evap_rate)
        src_mass = src_mass + (mass_now - shrunk)
        src_energy = src_energy - drop_dt * heat_flow * mass_now
        temp_now = temp_now + drop_dt * (heat_flow - latent_coef * evap_rate)
        mass_now = shrunk
    return mass_now, temp_now, src_mass, src_energy


def kernel(
    n_gx, side,
    gas_hbm, kappa_hbm, vel_hbm, mass_hbm, temp_hbm, fill_hbm, cell_hbm, dest_hbm,
    gas_out, mass_out, temp_out,
    gas, kappa, vel, mass, temp, fill, cell, dest, dest_s,
    tables, outgo, relay, arrive, halo_x, halo_y, picked,
    in_sem, ready_z, ready_x, ready_d,
    gp_send, dp_send, g1_send, g1_recv, d1_send, d1_recv, g2_send, g2_recv, d2_send, d2_recv, halo_send, halo_recv,
):
    n_yz = side * side
    gx = lax.axis_index("gx")
    me = lax.axis_index("yz")
    me_x, me_z = me // side, me % side
    nfield = gas.shape[0]
    blocks = mass.shape[0]
    half = SUB // 2
    has_xm, has_xp = gx > 0, gx < n_gx - 1
    has_ym, has_yp = me > 0, me < n_yz - 1
    wrap_up = jnp.logical_and(me_z == side - 1, has_yp)
    wrap_down = jnp.logical_and(me_z == 0, has_ym)

    one = jnp.int32(1)
    zero = jnp.int32(0)

    late_z = jnp.where(jnp.logical_and(gx == 0, me_x == 0), one, zero)
    late_x = jnp.where(jnp.logical_and(gx == 0, me_z == 0), one, zero)
    is_late = jnp.logical_and(gx == 0, me == 0)
    past_corner = jnp.logical_and(jnp.logical_and(gx == 0, me_x == 0), me_z > 0)
    by_corner = jnp.logical_and(jnp.logical_and(gx == 0, me_z == 0), me_x > 0)

    def rank_z(z):
        late = jnp.where(z == 0, side - 2, jnp.where(z == side - 1, side - 1, z - 1))
        return jnp.where(late_z == 1, late, z)

    def turn_z(t):
        late = jnp.where(t == side - 2, 0, jnp.where(t == side - 1, side - 1, t + 1))
        return jnp.where(is_late, t, jnp.where(late_z == 1, late, t))

    def rank_x(x):
        return (jnp.where(x < side // 2, x, side // 2 + side - 1 - x) + side - late_x) % side

    my_rank = rank_x(me_x)
    my_turn = rank_z(me_z)

    def signal(sem, where):
        pl.semaphore_signal(sem, inc=1, device_id=where, device_id_type=MESH)

    loads = [
        pltpu.make_async_copy(src, dst, in_sem.at[i])
        for i, (src, dst) in enumerate(
            (
                (gas_hbm.at[0], tables.at[me_z, me_x, 0]),
                (gas_hbm.at[nfield - 1], tables.at[me_z, me_x, 1]),
                (dest_hbm, dest), (fill_hbm, fill), (cell_hbm, cell), (mass_hbm, mass),
                (temp_hbm, temp), (dest_hbm, dest_s),
                (gas_hbm, gas), (kappa_hbm, kappa), (vel_hbm, vel),
            )
        )
    ]
    for load in loads:
        load.start()

    halo_x[...] = jnp.zeros_like(halo_x)
    halo_y[...] = jnp.zeros_like(halo_y)

    barrier = pltpu.get_barrier_semaphore()

    @pl.when(has_xm)
    def _():
        signal(barrier, {"gx": gx - 1})

    @pl.when(has_xp)
    def _():
        signal(barrier, {"gx": gx + 1})

    def greet_z(z, carry):
        @pl.when(rank_z(z) > my_turn)
        def _():
            signal(barrier, {"yz": me_x * side + z})

        return carry

    def greet_x(x, carry):
        @pl.when(rank_x(x) > my_rank)
        def _():
            signal(barrier, {"yz": x * side + me_z})

        return carry

    lax.fori_loop(0, side, greet_z, 0)
    lax.fori_loop(0, side, greet_x, 0)

    @pl.when(by_corner)
    def _():
        def greet(z, carry):
            signal(barrier, {"yz": z})
            return carry

        lax.fori_loop(1, side, greet, 0)

    @pl.when(wrap_down)
    def _():
        signal(barrier, {"yz": me - 1})

    for load in loads[2:8]:
        load.wait()
    row_i = lax.broadcasted_iota(jnp.int32, (blocks, blocks), 0)
    col_i = lax.broadcasted_iota(jnp.int32, (blocks, blocks), 1)
    dest_row = jnp.broadcast_to(dest[...], (blocks, blocks)).astype(F32)
    fill_row = jnp.broadcast_to(fill[...], (blocks, blocks)).astype(F32)
    dest_col = jnp.sum(jnp.where(row_i == col_i, dest_row, 0.0), axis=1, keepdims=True)
    fill_col = jnp.sum(jnp.where(row_i == col_i, fill_row, 0.0), axis=1, keepdims=True)
    same = jnp.where(dest_row == dest_col, 1.0, 0.0)
    rank_row = jnp.sum(jnp.where(row_i < col_i, same, 0.0), axis=0, keepdims=True)
    swapped_dest = (dest[...] % side) * side + dest[...] // side
    slot_row = rank_row * n_yz + swapped_dest.astype(F32)
    total = SLOTS * n_yz
    pick_slot = jnp.where(
        lax.broadcasted_iota(jnp.int32, (total, blocks), 0).astype(F32) == slot_row, 1.0, 0.0
    ).astype(BF16)
    lane = lax.broadcasted_iota(jnp.int32, (blocks, LANES), 1).astype(F32)
    living = lane < fill_col
    code = jnp.where(living, cell[...] + 1, 0).astype(F32)
    packed = jnp.concatenate([mass[...], temp[...], code], axis=1)
    placed = sum(
        jnp.dot(pick_slot, part, preferred_element_type=F32) for part in split3(packed)
    )
    for kind in range(3):
        for slot in range(SLOTS):
            for z in range(side):
                start = slot * n_yz + z * side
                outgo[z * ROWS + kind * SLOTS + slot] = placed[
                    start : start + side, kind * LANES : (kind + 1) * LANES
                ]

    pl.semaphore_wait(
        barrier,
        my_turn + my_rank + jnp.where(has_xm, one, zero) + jnp.where(has_xp, one, zero)
        + jnp.where(wrap_up, one, zero) + jnp.where(past_corner, side - 1, 0),
    )
    for load in loads[:2]:
        load.wait()

    def remote(src, dst, send_sem, recv_sem, where):
        return pltpu.make_async_remote_copy(
            src_ref=src, dst_ref=dst, send_sem=send_sem, recv_sem=recv_sem,
            device_id=where, device_id_type=MESH,
        )

    def kinds(z):
        return pl.ds(z * ROWS, ROWS)

    def gas_along_z(z):
        mine = tables.at[me_z, me_x]
        return remote(mine, mine, g1_send, g1_recv.at[me_z], {"yz": me_x * side + z})

    def drops_along_z(z):
        return remote(outgo.at[kinds(z)], relay.at[kinds(me_z)], d1_send, d1_recv.at[me_z], {"yz": me_x * side + z})

    def gas_along_x(z, x):
        tile = tables.at[z, me_x]
        return remote(tile, tile, g2_send, g2_recv.at[z], {"yz": x * side + me_z})

    def drops_along_x(z, x):
        return remote(
            relay.at[kinds(z), x], arrive.at[kinds(z), me_x],
            d2_send, d2_recv.at[z], {"yz": x * side + me_z},
        )

    def early_gas(z, carry):
        @pl.when(rank_z(z) < my_turn)
        def _():
            gas_along_z(z).start()

        return carry

    lax.fori_loop(0, side, early_gas, 0)

    def gas_past(x):
        tile = tables.at[me_z, me_x]
        return remote(tile, tile, gp_send, g2_recv.at[me_z], {"yz": x * side})

    def drops_past(x):
        return remote(
            outgo.at[kinds(0), x], arrive.at[kinds(me_z), me_x], dp_send, d2_recv.at[me_z], {"yz": x * side}
        )

    def past(make):
        @pl.when(past_corner)
        def _():
            def send(x, carry):
                make(x).start()
                return carry

            lax.fori_loop(1, side, send, 0)

    past(gas_past)

    def early_drops(z, carry):
        @pl.when(rank_z(z) < my_turn)
        def _():
            drops_along_z(z).start()

        return carry

    lax.fori_loop(0, side, early_drops, 0)
    past(drops_past)

    def tell_z(z, carry):
        @pl.when(rank_z(z) < my_turn)
        def _():
            signal(ready_z.at[me_z], {"yz": me_x * side + z})

        return carry

    def tell_x(x, carry):
        @pl.when(rank_x(x) < my_rank)
        def _():
            signal(ready_x.at[me_x], {"yz": x * side + me_z})

        return carry

    lax.fori_loop(0, side, tell_z, 0)
    lax.fori_loop(0, side, tell_x, 0)

    @pl.when(wrap_up)
    def _():
        signal(ready_d, {"yz": me + 1})


    for load in loads[8:]:
        load.wait()

    def halo_copy(src, dst, index, where):
        return remote(src, dst, halo_send.at[index], halo_recv.at[index], where)

    to_xp = [halo_copy(gas.at[:, half:SUB], halo_x.at[:, 0:half], 0, {"gx": gx + 1})]
    to_xm = [halo_copy(gas.at[:, 0:half], halo_x.at[:, half:SUB], 1, {"gx": gx - 1})]
    to_yp = [
        halo_copy(gas.at[:, pl.ds(g + half - 1, 1)], halo_y.at[:, pl.ds(g, 1)], 2 + i, {"yz": me + 1})
        for i, g in enumerate((0, half))
    ]
    to_ym = [
        halo_copy(gas.at[:, pl.ds(g, 1)], halo_y.at[:, pl.ds(g + half - 1, 1)], 4 + i, {"yz": me - 1})
        for i, g in enumerate((0, half))
    ]

    def start_if(condition, copies):
        @pl.when(condition)
        def _():
            for copy in copies:
                copy.start()

    start_if(has_xp, to_xp)
    start_if(has_xm, to_xm)
    start_if(wrap_up, to_yp)
    up_z, down_z = me_z < side - 1, me_z > 0
    start_if(jnp.logical_and(up_z, rank_z(me_z + 1) < my_turn), to_yp)
    start_if(jnp.logical_and(down_z, rank_z(me_z - 1) < my_turn), to_ym)
    relay[kinds(me_z)] = outgo[kinds(me_z)]

    def await_x(x, carry):
        @pl.when(jnp.logical_and(rank_x(x) > my_rank, jnp.logical_not(jnp.logical_and(by_corner, x == 0))))
        def _():
            pl.semaphore_wait(ready_x.at[x], 1)

        return carry

    lax.fori_loop(0, side, await_x, 0)

    def send_to(z, above):
        @pl.when(rank_z(z) > above)
        def _():
            pl.semaphore_wait(ready_z.at[z], 1)
            gas_along_z(z).start()
            drops_along_z(z).start()

        start_if(jnp.logical_and(z == me_z + 1, rank_z(z) > above), to_yp)
        start_if(jnp.logical_and(z == me_z - 1, rank_z(z) > above), to_ym)

    def step_on(z):
        send_to(z, my_turn + 2)

        @pl.when(z != me_z)
        def _():
            remote(
                tables.at[z, me_x], tables.at[z, me_x], g1_send, g1_recv.at[z], {"yz": me}
            ).wait_recv()

        relays = jnp.logical_or(jnp.logical_not(is_late), z == me_z)
        first = jnp.where(by_corner, one, zero)

        def forward_gas(x, carry):
            @pl.when(jnp.logical_and(x != me_x, relays))
            def _():
                gas_along_x(z, x).start()

            return carry

        lax.fori_loop(first, side, forward_gas, 0)

        @pl.when(z != me_z)
        def _():
            remote(relay.at[kinds(z)], relay.at[kinds(z)], d1_send, d1_recv.at[z], {"yz": me}).wait_recv()

        def forward_drops(x, carry):
            @pl.when(jnp.logical_and(x != me_x, relays))
            def _():
                drops_along_x(z, x).start()

            return carry

        lax.fori_loop(first, side, forward_drops, 0)
        arrive[kinds(z), pl.ds(me_x, 1), :] = relay[kinds(z), pl.ds(me_x, 1), :]

    def bulk(view, sem):
        return pltpu.make_async_copy(view, view, sem)

    row_ids = lax.broadcasted_iota(jnp.int32, (LANES, LANES), 0)
    up_rows = lax.broadcasted_iota(jnp.int32, (SUB, LANES), 0)

    def group_in(z):
        bulk(arrive.at[kinds(z), pl.ds(0, side - 1)], d2_recv.at[z]).wait()

        def kind_of(kind):
            return jnp.concatenate(
                [
                    arrive[z * ROWS + kind * SLOTS + slot]
                    for slot in range(SLOTS)
                ],
                axis=0,
            )

        mass_in, temp_in = kind_of(0), kind_of(1)
        place = kind_of(2).astype(jnp.int32) - 1
        lower = place & (LANES - 1)
        upper = place >> 7
        fuel_gas = jnp.zeros_like(mass_in)
        temp_gas = jnp.zeros_like(mass_in)
        fuel_field = tables[me_z, me_x, 0]
        temp_field = tables[me_z, me_x, 1]
        for u in range(SUB):
            here = upper == u
            fuel_row = jnp.broadcast_to(fuel_field[u : u + 1], mass_in.shape)
            temp_row = jnp.broadcast_to(temp_field[u : u + 1], mass_in.shape)
            fuel_gas = jnp.where(
                here, jnp.take_along_axis(fuel_row, lower, axis=1, mode="promise_in_bounds"), fuel_gas
            )
            temp_gas = jnp.where(
                here, jnp.take_along_axis(temp_row, lower, axis=1, mode="promise_in_bounds"), temp_gas
            )
        return mass_in, temp_in, fuel_gas, temp_gas, lower, upper

    def deposit(lower, upper, src_mass, src_energy):
        values = []
        for value in (src_mass, src_energy):
            high = value.astype(BF16).astype(F32)
            values += [high, value - high]
        hots, weighted = [], []
        for b in range(lower.shape[0]):
            hots.append(jnp.where(lower[b : b + 1] == row_ids, 1.0, 0.0).astype(BF16))
            here = upper[b : b + 1] == up_rows
            weighted.append(
                jnp.concatenate([jnp.where(here, v[b : b + 1], 0.0) for v in values], axis=0).astype(BF16)
            )
        return lax.dot_general(
            jnp.concatenate(weighted, axis=1), jnp.concatenate(hots, axis=1),
            (((1,), (1,)), ((), ())), preferred_element_type=F32,
        )

    def group(z):
        mass_in, temp_in, fuel_gas, temp_gas, lower, upper = group_in(z)
        _, _, src_mass, src_energy = droplet_step(mass_in, temp_in, fuel_gas, temp_gas)
        return deposit(lower, upper, src_mass, src_energy)

    def gas_ready(z):
        bulk(tables.at[z, pl.ds(0, side - 1)], g2_recv.at[z]).wait()

    def to_corner(z, carry):
        gas_along_x(z, 0).start()
        drops_along_x(z, 0).start()
        return carry

    for ahead in (1, 2):

        @pl.when(my_turn + ahead < side)
        def _(ahead=ahead):
            send_to(turn_z(my_turn + ahead), my_turn)

    def advance(t, carry):
        step_on(turn_z(t))

        @pl.when(jnp.logical_and(by_corner, t == side - 2))
        def _():
            pl.semaphore_wait(ready_x.at[0], 1)
            lax.fori_loop(0, side - 1, to_corner, 0)

        @pl.when(jnp.logical_and(by_corner, t == side - 1))
        def _():
            to_corner(side - 1, 0)

        return carry

    lax.fori_loop(0, side, advance, 0)

    summed = lax.fori_loop(
        0, side - 1, lambda z, summed: summed + group(z), jnp.zeros((4 * SUB, LANES), F32)
    )

    @pl.when(wrap_down)
    def _():
        pl.semaphore_wait(ready_d, 1)
        for copy in to_ym:
            copy.start()

    for exists, copies in ((has_xm, to_xp), (has_xp, to_xm), (has_ym, to_yp), (has_yp, to_ym)):

        @pl.when(exists)
        def _(copies=copies):
            for copy in copies:
                copy.wait_recv()

    sub_id = lax.broadcasted_iota(jnp.int32, (SUB, LANES), 0)
    lane_id = lax.broadcasted_iota(jnp.int32, (SUB, LANES), 1)
    first_x = sub_id < half
    first_y, last_y = sub_id % half == 0, sub_id % half == half - 1
    first_z, last_z = lane_id == 0, lane_id == LANES - 1
    kap, velo = kappa[...], vel[...]
    ends = {}
    for f in range(nfield):
        field, hx, hy = gas[f], halo_x[f], halo_y[f]
        swapped = pltpu.roll(field, half, 0)
        before_x = jnp.where(first_x, hx, swapped)
        after_x = jnp.where(first_x, swapped, hx)
        before_y = jnp.where(first_y, hy, pltpu.roll(field, 1, 0))
        after_y = jnp.where(last_y, hy, pltpu.roll(field, SUB - 1, 0))
        before_z = jnp.where(first_z, field, pltpu.roll(field, 1, 1))
        after_z = jnp.where(last_z, field, pltpu.roll(field, LANES - 1, 1))
        beside = after_x + before_x + after_y + before_y + after_z + before_z
        moved = field + kap * (beside - 6.0 * field) - velo * (field - before_x)
        if f in (0, nfield - 1):
            ends[f] = moved
        else:
            gas_out[f] = moved

    for z in range(side):
        gas_ready(z)
    for j in range(blocks):
        target = dest_s[0, j]
        z, x = target % side, target // side
        for kind in range(2):
            picked[kind, pl.ds(j * SUB, SUB), :] = tables[z, x, kind]
    own_lower = cell[...] & (LANES - 1)
    own_upper = cell[...] >> 7
    own_gas = []
    for kind in range(2):
        found = jnp.zeros((blocks, LANES), F32)
        for u in range(SUB):
            row = picked[kind, pl.ds(u, blocks, stride=SUB), :]
            looked = jnp.take_along_axis(row, own_lower, axis=1, mode="promise_in_bounds")
            found = jnp.where(own_upper == u, looked, found)
        own_gas.append(found)
    mass_in, temp_in, fuel_gas, temp_gas, lower, upper = group_in(side - 1)
    _, _, src_mass, src_energy = droplet_step(mass_in, temp_in, fuel_gas, temp_gas)
    own_mass, own_temp, _, _ = droplet_step(mass[...], temp[...], own_gas[0], own_gas[1])
    mass_out[...] = jnp.where(living, own_mass, 0.0)
    temp_out[...] = jnp.where(living, own_temp, 0.0)
    summed = summed + deposit(lower, upper, src_mass, src_energy)
    gas_out[0] = ends[0] + (summed[0:SUB] + summed[SUB : 2 * SUB])
    gas_out[nfield - 1] = ends[nfield - 1] + (summed[2 * SUB : 3 * SUB] + summed[3 * SUB : 4 * SUB])

    bulk(tables.at[0, pl.ds(0, side - 1)], g1_send).wait()
    bulk(outgo.at[pl.ds(0, (side - 1) * ROWS)], d1_send).wait()

    @pl.when(is_late)
    def _():
        bulk(tables.at[0, pl.ds(0, side - 1)], g2_send).wait()
        bulk(arrive.at[kinds(0), pl.ds(0, side - 1)], d2_send).wait()

    @pl.when(jnp.logical_not(is_late))
    def _():
        bulk(tables.at[pl.ds(0, side - 1)], g2_send).wait()
        bulk(arrive.at[:, pl.ds(0, side - 1)], d2_send).wait()

    @pl.when(past_corner)
    def _():
        bulk(tables.at[0, pl.ds(0, side - 1)], gp_send).wait()
        bulk(arrive.at[kinds(0), pl.ds(0, side - 1)], dp_send).wait()

    for exists, copies in ((has_xp, to_xp), (has_xm, to_xm), (has_yp, to_yp), (has_ym, to_ym)):

        @pl.when(exists)
        def _(copies=copies):
            for copy in copies:
                copy.wait_send()


def emit(gas_in, mass_in, temp_in, gas_out, mass_out, temp_out, sems):
    copies = [
        pltpu.make_async_copy(src, dst, sems.at[i])
        for i, (src, dst) in enumerate(((gas_in, gas_out), (mass_in, mass_out), (temp_in, temp_out)))
    ]
    for copy in copies:
        copy.start()
    for copy in copies:
        copy.wait()


def solution(mesh):
    n_gx, n_yz = mesh.shape["gx"], mesh.shape["yz"]
    side = math.isqrt(n_yz)
    assert side * side == n_yz

    def body(gas, kappa, velocity, drop_mass, drop_temp, block_fill, drop_cell, block_dest):
        nfield, cx, cy, cz = gas.shape
        blocks = drop_mass.shape[0]
        any_spec = pl.BlockSpec(memory_space=pl.ANY)
        vmem_spec = pl.BlockSpec(memory_space=pltpu.VMEM)
        tile = (cx * cy, cz)
        dma = pltpu.SemaphoreType.DMA
        regular = pltpu.SemaphoreType.REGULAR
        gas_next, mass_next, temp_next = pl.pallas_call(
            functools.partial(kernel, n_gx, side),
            out_shape=(
                pltpu.VMEM((nfield,) + tile, F32),
                pltpu.VMEM(drop_mass.shape, F32),
                pltpu.VMEM(drop_mass.shape, F32),
            ),
            in_specs=[any_spec] * 8,
            out_specs=(vmem_spec,) * 3,
            scratch_shapes=[
                pltpu.VMEM((nfield,) + tile, F32),
                pltpu.VMEM(tile, F32),
                pltpu.VMEM(tile, F32),
                pltpu.VMEM((blocks, LANES), F32),
                pltpu.VMEM((blocks, LANES), F32),
                pltpu.VMEM((1, blocks), jnp.int32),
                pltpu.VMEM((blocks, LANES), jnp.int32),
                pltpu.VMEM((1, blocks), jnp.int32),
                pltpu.SMEM((1, blocks), jnp.int32),
                pltpu.VMEM((side, side, 2) + tile, F32),
                pltpu.VMEM((side * ROWS, side, LANES), F32),
                pltpu.VMEM((side * ROWS, side, LANES), F32),
                pltpu.VMEM((side * ROWS, side, LANES), F32),
                pltpu.VMEM((nfield,) + tile, F32),
                pltpu.VMEM((nfield,) + tile, F32),
                pltpu.VMEM((2, blocks * SUB, LANES), F32),
                dma((11,)),
                regular((side,)),
                regular((side,)),
                regular,
                dma, dma,
                dma, dma((side,)), dma, dma((side,)),
                dma, dma((side,)), dma, dma((side,)),
                dma((6,)), dma((6,)),
            ],
            compiler_params=pltpu.CompilerParams(collective_id=0, has_side_effects=True),
            name="spray_step",
        )(
            gas.reshape((nfield,) + tile),
            kappa.reshape(tile),
            velocity.reshape(tile),
            drop_mass,
            drop_temp,
            block_fill.reshape(1, blocks),
            drop_cell,
            block_dest.reshape(1, blocks),
        )
        gas_next, mass_next, temp_next = pl.pallas_call(
            emit,
            out_shape=(
                jax.ShapeDtypeStruct((nfield,) + tile, F32),
                jax.ShapeDtypeStruct(drop_mass.shape, F32),
                jax.ShapeDtypeStruct(drop_mass.shape, F32),
            ),
            in_specs=(vmem_spec,) * 3,
            out_specs=(any_spec,) * 3,
            scratch_shapes=[dma((3,))],
            name="emit",
        )(*(pltpu.with_memory_space_constraint(a, pltpu.VMEM) for a in (gas_next, mass_next, temp_next)))
        return gas_next.reshape(gas.shape), mass_next, temp_next

    in_specs = (
        P(None, "gx", "yz", None),
        P("gx", "yz", None),
        P("gx", "yz", None),
        P(("gx", "yz"), None),
        P(("gx", "yz"), None),
        P(("gx", "yz")),
        P(("gx", "yz"), None),
        P(("gx", "yz"), None),
    )
    out_specs = (P(None, "gx", "yz", None), P(("gx", "yz"), None), P(("gx", "yz"), None))
    return jax.shard_map(body, mesh=mesh, in_specs=in_specs, out_specs=out_specs, check_vma=False)
```
